256 devices in a mesh: req: 16 (over y_hi, x, core), tp: 16 (over y_lo, z).
Axes of the slice: x: 4, y: 4 (y_hi: 2, y_lo: 2; y = y_hi * 2 + y_lo), z: 8, core: 2. Of those that a mesh axis runs over, the one named last changes fastest.
Arguments:
- tokens: bfloat16 [14336, 5120], P(('req', 'tp')), may hold values from -6 to 6
- qkv_weight: bfloat16 [5120, 3, 4096], P('req', None, 'tp')
- out_weight: bfloat16 [4096, 5120], P('tp', 'req')
- query_key_gain: float32 [2, 4096], P(None, 'tp'), may hold values from 0.25 to 1.75
- post_gain: float32 [5120], replicated, may hold values from 0.25 to 1.75
- pool_cache: bfloat16 [512, 128, 2, 4096], P('req', None, None, 'tp'), may hold values from -68 to 68
- lengths: int32 [16, 16], P('req'), may hold values from 1 to 256, 896 in all within a row
- prefix_pages: int32 [16, 16], P('req'), may hold values from 1 to 16, 32 in all within a row
- pool_order: int32 [16, 32], P('req'), may hold values from 0 to 31, each once within a row
- owners: int32 [16, 16], P('req'), may hold values from 0 to 15, each once within a row
Outputs:
- hidden: bfloat16 [14336, 5120], P(('req', 'tp'))
- handed_pages: bfloat16 [512, 128, 2, 4096], P('req', None, None, 'tp')
The draws below stay inside these ranges and needn't reach their ends.
Inputs may be any that keep to these rules, and one draw needn't show every extreme that they name: `lengths`: each row sums to 896; the largest entry of every row is exactly 256. `prefix_pages`: each row sums to 32; the largest entry of every row is exactly 16. `pool_order`: each row names every slot once. `owners`: each row names every owner once.
All inputs are finite; a program needn't handle non-finite values.
Results may differ from the reference program's by a relative error of at most 0.014.
Values may be sent and summed in bfloat16 or wider, within the bound.
A program may use at most 128 MiB of HBM per device.

```python
import math
import jax
import jax.numpy as jnp
import numpy as np
from jax import lax

D = 5120
HEADS = 32
HEAD = 128
PAGE = 128
CAP = 2
BLOCK = 896
REQS = 16
POOL = 32
PMAX = 16
HD = 4096
TOKENS = 14336
N_REQ = 16
N_TP = 16


def draw_qkv_weight(key, part):
    normal_part = jnp.clip(jax.random.normal(key, (D, 3, HD), jnp.float32), -6.0, 6.0)
    head_index = (jnp.arange(HD) // HEAD).astype(jnp.float32)
    rising = 3.0 ** (head_index / max(HEADS - 1, 1))
    column_scale = jnp.stack([rising, rising, jnp.ones_like(rising)])
    return (normal_part * column_scale[None, :, :] / math.sqrt(D)).astype(jnp.bfloat16)


def draw_out_weight(key, part):
    normal_part = jnp.clip(jax.random.normal(key, (HD, D), jnp.float32), -6.0, 6.0)
    column_index = jnp.arange(D).astype(jnp.float32)
    rising = 3.0 ** (column_index / max(D - 1, 1))
    return (normal_part * rising[None, :] / math.sqrt(HD)).astype(jnp.bfloat16)


def draw_pool_cache(key, part):
    shape_all = (N_REQ * POOL, PAGE, 2, HD)
    return jnp.clip(jax.random.normal(key, shape_all, jnp.float32), -6.0, 6.0).astype(jnp.bfloat16)


def levels(stream_key, extent, pieces, least, high):
    loudness = 1.0
    for axis_at, shards_of in pieces:
        steps = jax.random.uniform(jax.random.fold_in(jax.random.fold_in(stream_key, 6), axis_at), (shards_of,), jnp.float32, least / len(pieces), high / len(pieces))
        loudness = loudness * jnp.repeat(jnp.exp(steps), extent[axis_at] // shards_of).reshape((-1,) + (1,) * (len(extent) - 1 - axis_at))
    return loudness


def split_up(amount, total, limit, slope):
    loads = [(1 << 20) // math.isqrt(grade ** slope) + 1 for grade in range(2, amount + 1)]
    rest, given = total - limit - (amount - 1), [1] * (amount - 1)
    while rest > 0:
        free = [i for i in range(amount - 1) if given[i] < limit]
        pool, left = sum([loads[i] for i in free]), rest
        for i in free:
            more = min(limit - given[i], max(1, left * loads[i] // pool), rest)
            given[i] = given[i] + more
            rest = rest - more
    return np.array([limit] + given)


def ragged_sizes(stream_key, count, total, limit, lean):
    if count == 2:
        one = jax.random.randint(stream_key, (), max(1, total - limit), min(limit, total - 1) + 1)
        return jnp.stack([one, total - one])
    tallies = jnp.asarray(split_up(count, total, limit, lean), jnp.int32)
    couples = (count - 1) // 2
    source_of, receiver = tallies[1:1 + 2 * couples:2], tallies[2:2 + 2 * couples:2]
    slack = jnp.minimum(source_of - 1, limit - receiver)
    shifted = jax.random.randint(jax.random.fold_in(stream_key, 1), (couples,), 0, 1 << 20) % (slack + 1)
    tallies = tallies.at[1:1 + 2 * couples:2].set(source_of - shifted).at[2:2 + 2 * couples:2].set(receiver + shifted)
    return tallies[jax.random.permutation(jax.random.fold_in(stream_key, 2), count)]


def scatter_about(key, extent, width, bound, cuts=(), kind=jnp.bfloat16):
    result = width * jax.random.normal(key, extent, jnp.float32)
    if cuts:
        result = result * levels(key, extent, cuts, -0.22, 0.18)
    return jnp.clip(result, -bound, bound).astype(kind)


def setup_inputs(seed: int = 0) -> dict:
    arg_keys = jax.random.split(jax.random.key(seed), 11)
    return {
        "tokens": scatter_about(arg_keys[0], (TOKENS, D), 1.0, 6.0, ((0, 256),)),
        "qkv_weight": draw_qkv_weight(jax.random.fold_in(arg_keys[10], 71), 0),
        "out_weight": draw_out_weight(jax.random.fold_in(arg_keys[10], 71), 0),
        "query_key_gain": jnp.clip(1.0 + 0.15 * jax.random.normal(arg_keys[3], (2, HD), jnp.float32), 0.25, 1.75),
        "post_gain": jnp.clip(1.0 + 0.15 * jax.random.normal(arg_keys[4], (D,), jnp.float32), 0.25, 1.75),
        "pool_cache": draw_pool_cache(jax.random.fold_in(arg_keys[10], 71), 0),
        "lengths": jax.vmap(lambda own: ragged_sizes(own, REQS, BLOCK, CAP * PAGE, 2))(jax.random.split(arg_keys[6], N_REQ)).reshape((N_REQ, REQS)).astype(jnp.int32),
        "prefix_pages": jax.vmap(lambda own: ragged_sizes(own, REQS, POOL, PMAX, 2))(jax.random.split(arg_keys[7], N_REQ)).reshape((N_REQ, REQS)).astype(jnp.int32),
        "pool_order": jax.vmap(lambda own: jax.random.permutation(own, POOL))(jax.random.split(arg_keys[8], N_REQ)).reshape((N_REQ, POOL)).astype(jnp.int32),
        "owners": jax.vmap(lambda own: jax.random.permutation(own, N_REQ))(jax.random.split(arg_keys[9], N_REQ)).reshape((N_REQ, REQS)).astype(jnp.int32),
    }


norm_eps = 1e-06
rope_base = 500000.0
masked_score = -1e+30

def token_layout(lengths_row, prefix_row, block_len):
    ends_at = jnp.cumsum(lengths_row).astype(jnp.int32)
    starts_at = (ends_at - lengths_row).astype(jnp.int32)
    token_ids = jnp.arange(block_len, dtype=jnp.int32)
    request_of = lax.optimization_barrier(jnp.sum((token_ids[:, None] >= ends_at[None, :]).astype(jnp.int32), axis=1))
    one_hot = (request_of[:, None] == jnp.arange(lengths_row.shape[0], dtype=jnp.int32)[None, :]).astype(jnp.int32)
    shift_of = lax.optimization_barrier(jnp.sum(one_hot * (prefix_row * PAGE - starts_at)[None, :], axis=1))
    return (request_of, (token_ids + shift_of).astype(jnp.int32), starts_at)

def slot_owner(prefix_row, order_row):
    page_ends = jnp.cumsum(prefix_row).astype(jnp.int32)
    page_ids = jnp.arange(order_row.shape[0], dtype=jnp.int32)
    page_request = lax.optimization_barrier(jnp.sum((page_ids[:, None] >= page_ends[None, :]).astype(jnp.int32), axis=1))
    matches = (order_row[None, :] == page_ids[:, None]).astype(jnp.int32)
    return lax.optimization_barrier(jnp.sum(matches * page_request[None, :], axis=1))

def rotate_heads(tensor, positions):
    half_dim = HEAD // 2
    frequency = rope_base ** (-(2.0 * jnp.arange(half_dim, dtype=jnp.float32)) / HEAD)
    angles = positions.astype(jnp.float32)[:, None] * frequency[None, :]
    cosine = jnp.cos(angles)[:, None, :]
    sine_part = jnp.sin(angles)[:, None, :]
    first_half = tensor[..., :half_dim]
    second_half = tensor[..., half_dim:]
    return jnp.concatenate([first_half * cosine - second_half * sine_part, second_half * cosine + first_half * sine_part], axis=-1)

def attend_head(queries, pool_keys, pool_values, new_keys, new_values, pool_mask, block_mask):
    score_scale = HEAD ** (-0.5)
    pool_scores = jnp.dot(queries, pool_keys.T, preferred_element_type=jnp.float32) * score_scale
    block_scores = jnp.dot(queries, new_keys.T, preferred_element_type=jnp.float32) * score_scale
    pool_scores = jnp.where(pool_mask, pool_scores, masked_score)
    block_scores = jnp.where(block_mask, block_scores, masked_score)
    row_max = jnp.maximum(lax.optimization_barrier(jnp.max(pool_scores, axis=1)), lax.optimization_barrier(jnp.max(block_scores, axis=1)))
    pool_exp = jnp.exp(pool_scores - row_max[:, None])
    block_exp = jnp.exp(block_scores - row_max[:, None])
    row_total = lax.optimization_barrier(jnp.sum(pool_exp, axis=1)) + lax.optimization_barrier(jnp.sum(block_exp, axis=1))
    pool_weights = (pool_exp / row_total[:, None]).astype(jnp.bfloat16)
    block_weights = (block_exp / row_total[:, None]).astype(jnp.bfloat16)
    mixed_out = jnp.dot(pool_weights, pool_values, preferred_element_type=jnp.float32)
    mixed_out = mixed_out + jnp.dot(block_weights, new_values, preferred_element_type=jnp.float32)
    return mixed_out.astype(jnp.bfloat16)

def build_send(kv_new, lengths_row, starts_at, owner_row):
    page_span = CAP * PAGE
    owner_count = owner_row.shape[0]
    owner_ids = jnp.arange(owner_count, dtype=jnp.int32)
    owner_pick = (owner_row[None, :] == owner_ids[:, None]).astype(jnp.int32)
    start_of = lax.optimization_barrier(jnp.sum(owner_pick * starts_at[None, :], axis=1))
    length_of = lax.optimization_barrier(jnp.sum(owner_pick * lengths_row[None, :], axis=1))
    offsets = jnp.arange(page_span, dtype=jnp.int32)
    source = (start_of[:, None] + offsets[None, :]).astype(jnp.int32)
    is_valid = offsets[None, :] < length_of[:, None]
    source = jnp.clip(source, 0, kv_new.shape[0] - 1).reshape(-1)
    taken_rows = jnp.take(kv_new, source, axis=0).reshape(owner_count, page_span, kv_new.shape[1], kv_new.shape[2])
    return jnp.where(is_valid[:, :, None, None], taken_rows, jnp.zeros_like(taken_rows))

def reference(tokens, qkv_weight, out_weight, query_key_gain, post_gain, pool_cache, lengths, prefix_pages, pool_order, owners):
    flat_weight = qkv_weight.reshape(D, 3 * HD)
    group_width = HD // N_TP

    def run_batch(operands):
        rows_in, lengths_row, prefix_row, order_row, owner_row, pool_page = operands
        block_len = rows_in.shape[0]
        request_of, positions, starts_at = token_layout(lengths_row, prefix_row, block_len)
        joined_all = jnp.dot(rows_in, flat_weight, preferred_element_type=jnp.float32).reshape(block_len, 3, HD)
        queries = joined_all[:, 0]
        keys_raw = joined_all[:, 1]
        values_raw = joined_all[:, 2]
        queries = queries * lax.rsqrt(lax.optimization_barrier(jnp.mean(queries * queries, axis=1, keepdims=True)) + norm_eps) * query_key_gain[0]
        keys_raw = keys_raw * lax.rsqrt(lax.optimization_barrier(jnp.mean(keys_raw * keys_raw, axis=1, keepdims=True)) + norm_eps) * query_key_gain[1]
        query_rot = rotate_heads(queries.reshape(block_len, HEADS, HEAD), positions).astype(jnp.bfloat16)
        key_rot = rotate_heads(keys_raw.reshape(block_len, HEADS, HEAD), positions).astype(jnp.bfloat16)
        value_new = values_raw.reshape(block_len, HEADS, HEAD).astype(jnp.bfloat16)
        key_owner = jnp.repeat(slot_owner(prefix_row, order_row), PAGE)
        pool_mask = request_of[:, None] == key_owner[None, :]
        token_ids = jnp.arange(block_len, dtype=jnp.int32)
        block_mask = (request_of[:, None] == request_of[None, :]) & (token_ids[None, :] <= token_ids[:, None])
        pool_keys = pool_page[:, :, 0, :].reshape(POOL * PAGE, HEADS, HEAD)
        pool_values = pool_page[:, :, 1, :].reshape(POOL * PAGE, HEADS, HEAD)
        head_outs = lax.map(lambda per_head: attend_head(per_head[0], per_head[1], per_head[2], per_head[3], per_head[4], pool_mask, block_mask), (jnp.moveaxis(query_rot, 1, 0), jnp.moveaxis(pool_keys, 1, 0), jnp.moveaxis(pool_values, 1, 0), jnp.moveaxis(key_rot, 1, 0), jnp.moveaxis(value_new, 1, 0)))
        attention = jnp.moveaxis(head_outs, 0, 1).reshape(block_len, HD)

        def add_group(summed, group_index):
            head_cols = lax.dynamic_slice_in_dim(attention, group_index * group_width, group_width, 1)
            weight_rows = lax.dynamic_slice_in_dim(out_weight, group_index * group_width, group_width, 0)
            partial_out = jnp.dot(head_cols, weight_rows, preferred_element_type=jnp.float32).astype(jnp.bfloat16)
            return (summed + partial_out.astype(jnp.float32), group_index)
        projected = lax.scan(add_group, jnp.zeros((block_len, D), jnp.float32), jnp.arange(N_TP, dtype=jnp.int32))[0]
        post_scale = lax.rsqrt(lax.optimization_barrier(jnp.mean(projected * projected, axis=1, keepdims=True)) + norm_eps)
        hidden_rows = (rows_in.astype(jnp.float32) + projected * post_scale * post_gain[None, :]).astype(jnp.bfloat16)
        kv_new = jnp.stack([key_rot.reshape(block_len, HD), value_new.reshape(block_len, HD)], axis=1)
        outgoing = build_send(kv_new, lengths_row, starts_at, owner_row)
        return (hidden_rows, outgoing)
    batches = tokens.reshape(N_REQ, BLOCK, D)
    pool_batches = pool_cache.reshape(N_REQ, POOL, PAGE, 2, HD)
    hidden_all, outgoing_all = lax.map(run_batch, (batches, lengths, prefix_pages, pool_order, owners, pool_batches))
    handed_pages = jnp.swapaxes(outgoing_all, 0, 1).reshape(N_REQ * N_REQ * CAP, PAGE, 2, HD)
    return (hidden_all.reshape(TOKENS, D), handed_pages)
```

```python
import jax
import jax.numpy as jnp
from jax import lax
from jax.experimental import pallas as pl
from jax.experimental.pallas import tpu as pltpu
from jax.sharding import PartitionSpec as P

HEADS = 32
HEAD = 128
PAGE = 128
CAP = 2


norm_eps = 1e-06
rope_base = 500000.0
masked_score = -1e30


MESH = pl.DeviceIdType.MESH
ZN = 8
SPLIT = 32


def ring_place():
    tp = lax.axis_index("tp")
    sense = 1 - 2 * lax.rem(lax.axis_index("req"), 2)
    column = tp // ZN
    z = lax.rem(tp, ZN)

    def at(col, steps):
        return col * ZN + lax.rem(z + sense * steps + 4 * ZN, ZN)

    return tp, column, at


def greet(peers):
    barrier = pltpu.get_barrier_semaphore()
    for peer in peers:
        pl.semaphore_signal(barrier, inc=1, device_id={"tp": peer}, device_id_type=MESH)
    pl.semaphore_wait(barrier, len(peers))


def gather_kernel(tok_ref, out_ref, local_sem, send_sem, recv_sem):
    tp, col, at = ring_place()
    other = 1 - col
    right, left, across = at(col, 1), at(col, -1), at(other, 0)
    greet((right, left, across))
    rows = tok_ref.shape[0]
    head, tail, full = pl.ds(0, SPLIT), pl.ds(SPLIT, rows - SPLIT), pl.ds(0, rows)
    sends = []

    def push(src, origin, part, peer, slot):
        copy = pltpu.make_async_remote_copy(
            src_ref=src.at[part],
            dst_ref=out_ref.at[origin, part],
            send_sem=send_sem.at[slot],
            recv_sem=recv_sem.at[slot],
            device_id={"tp": peer},
            device_id_type=MESH,
        )
        copy.start()
        sends.append(copy)

    def arrive(origin, part, slot):
        pltpu.make_async_remote_copy(
            src_ref=out_ref.at[origin, part],
            dst_ref=out_ref.at[origin, part],
            send_sem=send_sem.at[slot],
            recv_sem=recv_sem.at[slot],
            device_id={"tp": across},
            device_id_type=MESH,
        ).wait_recv()

    push(tok_ref, tp, tail, across, 14)
    push(tok_ref, tp, full, right, 0)
    push(tok_ref, tp, full, left, 4)
    push(tok_ref, tp, head, across, 15)
    keep = pltpu.make_async_copy(tok_ref, out_ref.at[tp], local_sem)
    keep.start()
    arrive(across, tail, 14)
    push(out_ref.at[across], across, tail, right, 7)
    push(out_ref.at[across], across, tail, left, 11)
    for k in range(1, 5):
        origin = at(col, -k)
        arrive(origin, full, k - 1)
        if k < 4:
            push(out_ref.at[origin], origin, full, right, k)
        push(out_ref.at[origin], origin, head, across, 15 + k)
        if k < 4:
            origin = at(col, k)
            arrive(origin, full, 3 + k)
            if k < 3:
                push(out_ref.at[origin], origin, full, left, 4 + k)
            push(out_ref.at[origin], origin, head, across, 19 + k)
        origin = at(other, -k)
        arrive(origin, tail, 6 + k)
        if k < 4:
            push(out_ref.at[origin], origin, tail, right, 7 + k)
        if k < 4:
            origin = at(other, k)
            arrive(origin, tail, 10 + k)
            if k < 3:
                push(out_ref.at[origin], origin, tail, left, 11 + k)
    arrive(across, head, 15)
    for k in range(1, 5):
        arrive(at(other, -k), head, 15 + k)
        if k < 4:
            arrive(at(other, k), head, 19 + k)
    keep.wait()
    for copy in sends:
        copy.wait_send()


def gather_tokens(tokens):
    rows, width = tokens.shape
    out = pl.pallas_call(
        gather_kernel,
        out_shape=jax.ShapeDtypeStruct((2 * ZN, rows, width), tokens.dtype),
        in_specs=[pl.BlockSpec(memory_space=pltpu.VMEM)],
        out_specs=pl.BlockSpec(memory_space=pl.ANY),
        scratch_shapes=[
            pltpu.SemaphoreType.DMA,
            pltpu.SemaphoreType.DMA((23,)),
            pltpu.SemaphoreType.DMA((23,)),
        ],
        cost_estimate=pl.CostEstimate(flops=0, transcendentals=0, bytes_accessed=200000000),
        compiler_params=pltpu.CompilerParams(collective_id=0, has_side_effects=True),
    )(tokens)
    return out.reshape(2 * ZN * rows, width)


def sum_kernel(x_ref, out_ref, slots, send_sem, recv_sem):
    count = 2 * ZN
    tp = lax.axis_index("tp")
    peers = [lax.rem(tp + d, count) for d in range(1, count)]
    greet(peers)
    copies = []
    for d in range(1, count):
        copy = pltpu.make_async_remote_copy(
            src_ref=x_ref,
            dst_ref=slots.at[d],
            send_sem=send_sem.at[d],
            recv_sem=recv_sem.at[d],
            device_id={"tp": peers[d - 1]},
            device_id_type=MESH,
        )
        copy.start()
        copies.append(copy)
    for copy in copies:
        copy.wait()
    total = x_ref[...]
    for d in range(1, count):
        total = total + slots[d]
    out_ref[...] = total


def sum_over_tp(x):
    return pl.pallas_call(
        sum_kernel,
        out_shape=jax.ShapeDtypeStruct(x.shape, x.dtype),
        in_specs=[pl.BlockSpec(memory_space=pltpu.VMEM)],
        out_specs=pl.BlockSpec(memory_space=pltpu.VMEM),
        scratch_shapes=[
            pltpu.VMEM((2 * ZN,) + x.shape, x.dtype),
            pltpu.SemaphoreType.DMA((2 * ZN,)),
            pltpu.SemaphoreType.DMA((2 * ZN,)),
        ],
        cost_estimate=pl.CostEstimate(flops=0, transcendentals=0, bytes_accessed=20000000),
        compiler_params=pltpu.CompilerParams(collective_id=1, has_side_effects=True),
    )(x)


def token_layout(lengths_row, prefix_row, block_len):
    ends_at = jnp.cumsum(lengths_row)
    starts_at = ends_at - lengths_row
    token_ids = jnp.arange(block_len, dtype=jnp.int32)
    request_of = jnp.sum((token_ids[:, None] >= ends_at[None, :]).astype(jnp.int32), axis=1)
    one_hot = (
        request_of[:, None] == jnp.arange(lengths_row.shape[0], dtype=jnp.int32)[None, :]
    ).astype(jnp.int32)
    shift_of = jnp.sum(one_hot * (prefix_row * PAGE - starts_at)[None, :], axis=1)
    return (request_of, token_ids + shift_of, starts_at)


def slot_owner(prefix_row, order_row):
    page_ends = jnp.cumsum(prefix_row)
    page_ids = jnp.arange(order_row.shape[0], dtype=jnp.int32)
    page_request = jnp.sum((page_ids[:, None] >= page_ends[None, :]).astype(jnp.int32), axis=1)
    matches = (order_row[None, :] == page_ids[:, None]).astype(jnp.int32)
    return jnp.sum(matches * page_request[None, :], axis=1)


def rotate_heads(tensor, positions):
    half_dim = HEAD // 2
    frequency = rope_base ** (-(2.0 * jnp.arange(half_dim, dtype=jnp.float32)) / HEAD)
    angles = positions.astype(jnp.float32)[:, None] * frequency[None, :]
    cosine = jnp.cos(angles)[:, None, :]
    sine_part = jnp.sin(angles)[:, None, :]
    first_half = tensor[..., :half_dim]
    second_half = tensor[..., half_dim:]
    return jnp.concatenate(
        [
            first_half * cosine - second_half * sine_part,
            second_half * cosine + first_half * sine_part,
        ],
        axis=-1,
    )


def attend_head(queries, pool_keys, pool_values, new_keys, new_values, pool_mask, block_mask):
    score_scale = HEAD ** (-0.5)
    pool_scores = jnp.dot(queries, pool_keys.T, preferred_element_type=jnp.float32) * score_scale
    block_scores = jnp.dot(queries, new_keys.T, preferred_element_type=jnp.float32) * score_scale
    pool_scores = jnp.where(pool_mask, pool_scores, masked_score)
    block_scores = jnp.where(block_mask, block_scores, masked_score)
    row_max = jnp.maximum(jnp.max(pool_scores, axis=1), jnp.max(block_scores, axis=1))
    pool_exp = jnp.exp(pool_scores - row_max[:, None])
    block_exp = jnp.exp(block_scores - row_max[:, None])
    row_total = jnp.sum(pool_exp, axis=1) + jnp.sum(block_exp, axis=1)
    pool_weights = (pool_exp / row_total[:, None]).astype(jnp.bfloat16)
    block_weights = (block_exp / row_total[:, None]).astype(jnp.bfloat16)
    mixed_out = jnp.dot(pool_weights, pool_values, preferred_element_type=jnp.float32)
    mixed_out = mixed_out + jnp.dot(block_weights, new_values, preferred_element_type=jnp.float32)
    return mixed_out.astype(jnp.bfloat16)


def build_send(kv_new, lengths_row, starts_at, owner_row):
    page_span = CAP * PAGE
    owner_count = owner_row.shape[0]
    owner_ids = jnp.arange(owner_count, dtype=jnp.int32)
    owner_pick = (owner_row[None, :] == owner_ids[:, None]).astype(jnp.int32)
    start_of = jnp.sum(owner_pick * starts_at[None, :], axis=1)
    length_of = jnp.sum(owner_pick * lengths_row[None, :], axis=1)
    offsets = jnp.arange(page_span, dtype=jnp.int32)
    source = start_of[:, None] + offsets[None, :]
    is_valid = offsets[None, :] < length_of[:, None]
    source = jnp.where(is_valid, source, -1).reshape(-1)
    block_len = kv_new.shape[0]
    pick = (source[:, None] == jnp.arange(block_len, dtype=jnp.int32)[None, :]).astype(kv_new.dtype)
    flat = jnp.dot(
        pick, kv_new.reshape(block_len, -1), preferred_element_type=jnp.float32
    ).astype(kv_new.dtype)
    return flat.reshape(owner_count, page_span, kv_new.shape[1], kv_new.shape[2])


def hand_over(kv_new, lengths_row, starts_at, owner_row):
    outgoing = build_send(kv_new, lengths_row, starts_at, owner_row)
    arrived = lax.all_to_all(outgoing, "req", split_axis=0, concat_axis=0, tiled=True)
    return arrived.reshape(arrived.shape[0] * CAP, PAGE, arrived.shape[2], arrived.shape[3])


def body(
    tokens,
    qkv_weight,
    out_weight,
    query_key_gain,
    post_gain,
    pool_cache,
    lengths,
    prefix_pages,
    pool_order,
    owners,
):
    local_width = qkv_weight.shape[2]
    heads_here = local_width // HEAD
    block_tokens = gather_tokens(tokens)
    block_len = block_tokens.shape[0]
    flat_rows = qkv_weight.reshape(qkv_weight.shape[0], 3 * local_width)
    flat_piece = lax.all_gather(flat_rows, "req", axis=0, tiled=True)
    joined_all = jnp.dot(block_tokens, flat_piece, preferred_element_type=jnp.float32)
    joined_all = joined_all.reshape(block_len, 3, local_width)
    queries = joined_all[:, 0]
    keys_raw = joined_all[:, 1]
    values_raw = joined_all[:, 2]
    local_sums = jnp.stack(
        [jnp.sum(queries * queries, axis=1), jnp.sum(keys_raw * keys_raw, axis=1)]
    )
    global_sums = sum_over_tp(local_sums)
    inverse = lax.rsqrt(global_sums / (HEADS * HEAD) + norm_eps)
    queries = queries * inverse[0][:, None] * query_key_gain[0]
    keys_raw = keys_raw * inverse[1][:, None] * query_key_gain[1]
    lengths_row = lengths[0]
    prefix_row = prefix_pages[0]
    request_of, positions, starts_at = token_layout(lengths_row, prefix_row, block_len)
    query_rot = rotate_heads(queries.reshape(block_len, heads_here, HEAD), positions).astype(
        jnp.bfloat16
    )
    key_rot = rotate_heads(keys_raw.reshape(block_len, heads_here, HEAD), positions).astype(
        jnp.bfloat16
    )
    value_new = values_raw.reshape(block_len, heads_here, HEAD).astype(jnp.bfloat16)
    kv_new = jnp.stack(
        [key_rot.reshape(block_len, local_width), value_new.reshape(block_len, local_width)], axis=1
    )
    pool_count = pool_cache.shape[0]
    key_owner = jnp.repeat(slot_owner(prefix_row, pool_order[0]), PAGE)
    pool_mask = request_of[:, None] == key_owner[None, :]
    token_ids = jnp.arange(block_len, dtype=jnp.int32)
    block_mask = (request_of[:, None] == request_of[None, :]) & (
        token_ids[None, :] <= token_ids[:, None]
    )
    pool_keys = pool_cache[:, :, 0, :].reshape(pool_count * PAGE, heads_here, HEAD)
    pool_values = pool_cache[:, :, 1, :].reshape(pool_count * PAGE, heads_here, HEAD)
    head_outs = lax.map(
        lambda per_head: attend_head(
            per_head[0], per_head[1], per_head[2], per_head[3], per_head[4], pool_mask, block_mask
        ),
        (
            jnp.moveaxis(query_rot, 1, 0),
            jnp.moveaxis(pool_keys, 1, 0),
            jnp.moveaxis(pool_values, 1, 0),
            jnp.moveaxis(key_rot, 1, 0),
            jnp.moveaxis(value_new, 1, 0),
        ),
    )
    attention = jnp.moveaxis(head_outs, 0, 1).reshape(block_len, local_width)
    out_full = lax.all_gather(out_weight, "req", axis=1, tiled=True)
    projected = lax.psum_scatter(
        jnp.dot(attention, out_full, preferred_element_type=jnp.float32).astype(jnp.bfloat16),
        "tp",
        scatter_dimension=0,
        tiled=True,
    ).astype(jnp.float32)
    post_scale = lax.rsqrt(jnp.mean(projected * projected, axis=1, keepdims=True) + norm_eps)
    hidden = (tokens.astype(jnp.float32) + projected * post_scale * post_gain[None, :]).astype(
        jnp.bfloat16
    )
    handed_pages = hand_over(kv_new, lengths_row, starts_at, owners[0])
    return (hidden, handed_pages)


def solution(mesh):
    in_specs = (
        P(("req", "tp"), None),
        P("req", None, "tp"),
        P("tp", "req"),
        P(None, "tp"),
        P(),
        P("req", None, None, "tp"),
        P("req", None),
        P("req", None),
        P("req", None),
        P("req", None),
    )
    out_specs = (P(("req", "tp"), None), P("req", None, None, "tp"))
    return jax.shard_map(body, mesh=mesh, in_specs=in_specs, out_specs=out_specs, check_vma=False)
```
